32 devices in a mesh: shard: 4 (over y, x), ctx: 2 (over core), tp: 4 (over z).
Axes of the slice: x: 2, y: 2, z: 4, core: 2. Of those that a mesh axis runs over, the one named last changes fastest.
Arguments:
- tokens: bfloat16 [8192, 1024], P(('shard', 'ctx')), may hold values from -6 to 6
- segment_ids: int32 [4, 2048], P('shard'), may hold values from 0 to 3, never falling along the last dimension, each value on 1 to 1024 neighbouring positions
- cotangent: bfloat16 [8192, 1024], P(('shard', 'ctx')), may hold values from -6 to 6
- mixer_gain: float32 [1024], replicated, may hold values from 0.5 to 1.5
- query_weight: bfloat16 [1024, 1024], P('shard', 'tp'), may hold values from -0.1875 to 0.1875
- key_weight: bfloat16 [1024, 1024], P('shard', 'tp'), may hold values from -0.1875 to 0.1875
- value_weight: bfloat16 [1024, 2048], P('shard', 'tp'), may hold values from -0.1875 to 0.1875
- gate_weight: bfloat16 [1024, 2048], P('shard', 'tp'), may hold values from -0.1875 to 0.1875
- decay_weight: bfloat16 [1024, 8], P('shard', 'tp'), may hold values from -0.1875 to 0.1875
- beta_weight: bfloat16 [1024, 8], P('shard', 'tp'), may hold values from -0.1875 to 0.1875
- query_conv: float32 [4, 1024], P(None, 'tp'), may hold values from -2 to 2
- key_conv: float32 [4, 1024], P(None, 'tp'), may hold values from -2 to 2
- value_conv: float32 [4, 2048], P(None, 'tp'), may hold values from -2 to 2
- decay_log: float32 [8], P('tp'), may hold values from -7.6 to -2.3
- decay_bias: float32 [8], P('tp'), may hold values from -3 to 3
- out_gain: float32 [256], replicated, may hold values from 0.5 to 1.5
- output_weight: bfloat16 [2048, 1024], P('tp', 'shard'), may hold values from -0.1875 to 0.1875
- hidden_gain: float32 [1024], replicated, may hold values from 0.5 to 1.5
- hidden_gate: bfloat16 [1024, 2816], P('shard', 'tp'), may hold values from -0.1875 to 0.1875
- hidden_up: bfloat16 [1024, 2816], P('shard', 'tp'), may hold values from -0.1875 to 0.1875
- hidden_down: bfloat16 [2816, 1024], P('tp', 'shard'), may hold values from -0.15625 to 0.15625
Outputs:
- block_out: bfloat16 [8192, 1024], P(('shard', 'ctx'))
- input_grad: float32 [8192, 1024], P(('shard', 'ctx'))
- mixer_gain_grad: float32 [1024], replicated
- query_weight_grad: float32 [1024, 1024], P('shard', 'tp')
- key_weight_grad: float32 [1024, 1024], P('shard', 'tp')
- value_weight_grad: float32 [1024, 2048], P('shard', 'tp')
- gate_weight_grad: float32 [1024, 2048], P('shard', 'tp')
- decay_weight_grad: float32 [1024, 8], P('shard', 'tp')
- beta_weight_grad: float32 [1024, 8], P('shard', 'tp')
- query_conv_grad: float32 [4, 1024], P(None, 'tp')
- key_conv_grad: float32 [4, 1024], P(None, 'tp')
- value_conv_grad: float32 [4, 2048], P(None, 'tp')
- decay_log_grad: float32 [8], P('tp')
- decay_bias_grad: float32 [8], P('tp')
- out_gain_grad: float32 [256], replicated
- output_weight_grad: float32 [2048, 1024], P('tp', 'shard')
- hidden_gain_grad: float32 [1024], replicated
- hidden_gate_grad: float32 [1024, 2816], P('shard', 'tp')
- hidden_up_grad: float32 [1024, 2816], P('shard', 'tp')
- hidden_down_grad: float32 [2816, 1024], P('tp', 'shard')
The draws below stay inside these ranges and needn't reach their ends.
Inputs may be any that keep to these rules, and one draw needn't show every extreme that they name: `segment_ids`: within each packed row the document numbers never fall; each document has 1 to 1024 tokens and one has exactly 1024.
All inputs are finite; a program needn't handle non-finite values.
Results may differ from the reference program's by a relative error of at most 0.015.
The reference program's roundings to bfloat16 on the way count: a program that leaves them out, or rounds other values in their place, can miss the bound.
Values may be sent and summed in bfloat16 or wider, within the bound.
A program may use at most 256 MiB of HBM per device.

```python
import math
import jax
import jax.numpy as jnp
import numpy as np
from jax import lax

D = 1024
H = 8
DK = 128
DV = 256
FF = 2816
CONV = 4
GROUP = 64
ROW = 2048
TOKENS = 8192
HK = 1024
HV = 2048
SEGS = 4
SEG_MOST = 1024
N_SHARD = 4


def steps_of(own_key, extent, cuts, least, top_value):
    loudness, own = 1.0, jax.random.fold_in(own_key, 6)
    for axis_at, shards_of in cuts:
        steps = jnp.exp(jax.random.uniform(jax.random.fold_in(own, axis_at), (shards_of,), jnp.float32, least / len(cuts), top_value / len(cuts)))
        loudness = loudness * jnp.repeat(steps, extent[axis_at] // shards_of).reshape([-1 if axis == axis_at else 1 for axis in range(len(extent))])
    return loudness


def length_profile(count, total, bound, skew):
    loads = [(1 << 20) // math.isqrt(grade ** skew) + 1 for grade in range(2, count + 1)]
    surplus, counts = total - bound - (count - 1), [1] * (count - 1)
    while surplus > 0:
        movable = [i for i in range(count - 1) if counts[i] < bound]
        mass, remaining = sum([loads[i] for i in movable]), surplus
        for i in movable:
            more = min(bound - counts[i], max(1, remaining * loads[i] // mass), surplus)
            counts[i] = counts[i] + more
            surplus = surplus - more
    return np.array([bound] + counts)


def ragged_sizes(rng, amount, total, most, skew):
    if amount == 2:
        one = jax.random.randint(rng, (), max(1, total - most), min(most, total - 1) + 1)
        return jnp.stack([one, total - one])
    lengths = jnp.asarray(length_profile(amount, total, most, skew), jnp.int32)
    couples = (amount - 1) // 2
    source_of, receiver = lengths[1:1 + 2 * couples:2], lengths[2:2 + 2 * couples:2]
    room = jnp.minimum(source_of - 1, most - receiver)
    shifted = jax.random.randint(jax.random.fold_in(rng, 1), (couples,), 0, 1 << 20) % (room + 1)
    lengths = lengths.at[1:1 + 2 * couples:2].set(source_of - shifted).at[2:2 + 2 * couples:2].set(receiver + shifted)
    return lengths[jax.random.permutation(jax.random.fold_in(rng, 2), amount)]


def scatter_about(rng, shape, scale, bound, cuts=(), held_as=jnp.bfloat16):
    level = steps_of(rng, shape, cuts, -0.22, 0.18) if cuts else 1.0
    values = jax.random.normal(rng, shape, jnp.float32) * scale * level
    return jnp.minimum(jnp.maximum(values, -bound), bound).astype(held_as)


def setup_inputs(seed: int = 0) -> dict:
    key_list = jax.random.split(jax.random.key(seed), 22)
    tokens = scatter_about(key_list[0], (TOKENS, D), 1.0, 6.0, ((0, 8),))
    segment_ids = jax.vmap(lambda own: jnp.searchsorted(jnp.cumsum(ragged_sizes(own, SEGS, ROW, SEG_MOST, 0)), jnp.arange(ROW), side="right"))(jax.random.split(key_list[1], N_SHARD)).reshape((N_SHARD, ROW)).astype(jnp.int32)
    cotangent = scatter_about(key_list[2], (TOKENS, D), 1.0, 6.0, ((0, 8),))
    mixer_gain = jnp.clip(1.0 + 0.1 * jax.random.normal(key_list[3], (D,), jnp.float32), 0.5, 1.5)
    query_weight = scatter_about(key_list[4], (D, HK), D ** -0.5, 0.1875, ((0, 4), (1, 4)))
    key_weight = scatter_about(key_list[5], (D, HK), D ** -0.5, 0.1875, ((0, 4), (1, 4)))
    value_weight = scatter_about(key_list[6], (D, HV), D ** -0.5, 0.1875, ((0, 4), (1, 4)))
    gate_weight = scatter_about(key_list[7], (D, HV), D ** -0.5, 0.1875, ((0, 4), (1, 4)))
    decay_weight = scatter_about(key_list[8], (D, H), D ** -0.5, 0.1875, ((0, 4), (1, 4)))
    beta_weight = scatter_about(key_list[9], (D, H), D ** -0.5, 0.1875, ((0, 4), (1, 4)))
    query_conv = scatter_about(key_list[10], (CONV, HK), 0.5, 2.0, ((1, 4),), jnp.float32)
    key_conv = scatter_about(key_list[11], (CONV, HK), 0.5, 2.0, ((1, 4),), jnp.float32)
    value_conv = scatter_about(key_list[12], (CONV, HV), 0.5, 2.0, ((1, 4),), jnp.float32)
    decay_log = jnp.clip(-7.6 + 5.3 * jax.random.uniform(key_list[13], (H,), jnp.float32) ** steps_of(key_list[13], (H,), ((0, 4),), -0.2, 0.2), -7.6, -2.3)
    decay_bias = scatter_about(key_list[14], (H,), 1.0, 3.0, ((0, 4),), jnp.float32)
    out_gain = jnp.clip(1.0 + 0.1 * jax.random.normal(key_list[15], (DV,), jnp.float32), 0.5, 1.5)
    output_weight = scatter_about(key_list[16], (HV, D), (HV // 2) ** -0.5, 0.1875, ((0, 4), (1, 4)))
    hidden_gain = jnp.clip(1.0 + 0.1 * jax.random.normal(key_list[17], (D,), jnp.float32), 0.5, 1.5)
    hidden_gate = scatter_about(key_list[18], (D, FF), D ** -0.5, 0.1875, ((0, 4), (1, 4)))
    hidden_up = scatter_about(key_list[19], (D, FF), D ** -0.5, 0.1875, ((0, 4), (1, 4)))
    hidden_down = scatter_about(key_list[20], (FF, D), (FF // 2) ** -0.5, 0.15625, ((0, 4), (1, 4)))
    return {"tokens": tokens, "segment_ids": segment_ids, "cotangent": cotangent, "mixer_gain": mixer_gain, "query_weight": query_weight, "key_weight": key_weight, "value_weight": value_weight, "gate_weight": gate_weight, "decay_weight": decay_weight, "beta_weight": beta_weight, "query_conv": query_conv, "key_conv": key_conv, "value_conv": value_conv, "decay_log": decay_log, "decay_bias": decay_bias, "out_gain": out_gain, "output_weight": output_weight, "hidden_gain": hidden_gain, "hidden_gate": hidden_gate, "hidden_up": hidden_up, "hidden_down": hidden_down}


@jax.custom_vjp
def low(v):
    return lax.optimization_barrier(v.astype(jnp.bfloat16)).astype(jnp.float32)

@jax.custom_vjp
def low_back(v):
    return v

def low_keep(v):
    return (low(v), None)

def low_pass(kept, grad):
    return (grad,)

def back_keep(v):
    return (v, None)

def back_low(kept, grad):
    return (low(grad),)
low.defvjp(low_keep, low_pass)
low_back.defvjp(back_keep, back_low)
HIGH = lax.Precision.HIGHEST

def matmul(left, right):
    return jnp.dot(left, right, precision=HIGH, preferred_element_type=jnp.float32)

def rms_norm(values, gain):
    return values * lax.rsqrt(lax.optimization_barrier(jnp.mean(values * values, axis=-1, keepdims=True)) + 1e-06) * gain

def unit_rows(values):
    return values * lax.rsqrt(lax.optimization_barrier(jnp.sum(values * values, axis=-1, keepdims=True)) + 1e-06)

def short_conv(projected, weights, seg_pad, seg_row):
    length = projected.shape[0]
    padded = jnp.concatenate([jnp.zeros((CONV - 1, projected.shape[1]), jnp.float32), projected], axis=0)
    summed = jnp.zeros_like(projected)
    for offset in range(CONV):
        begin = CONV - 1 - offset
        linked = (seg_pad[begin:begin + length] == seg_row).astype(jnp.float32)
        summed = summed + weights[offset] * padded[begin:begin + length] * linked[:, None]
    return jax.nn.silu(summed)

def token_step(state, inputs):
    query, keys, values, beta, alpha = inputs
    state = alpha[:, None, None] * state
    guess = jnp.einsum('hvd,hd->hv', state, keys, precision=HIGH)
    state = state + beta[:, None, None] * jnp.einsum('hv,hd->hvd', values - guess, keys, precision=HIGH)
    return (state, jnp.einsum('hvd,hd->hv', state, query, precision=HIGH))

def block_scan(state, inputs):
    return lax.scan(token_step, state, inputs)

def delta_row(query, keys, values, beta, alpha):
    length = query.shape[0]
    blocks = length // GROUP

    def split(array):
        return array.reshape((blocks, GROUP) + array.shape[1:])
    start_state = jnp.zeros((H, DV, DK), jnp.float32)
    final_state, outputs = lax.scan(jax.checkpoint(block_scan), start_state, (split(query), split(keys), split(values), split(beta), split(alpha)))
    return outputs.reshape(length, H, DV)

def row_forward(x_row, seg_row, weights):
    mixer_gain, query_weight, key_weight, value_weight, gate_weight, decay_weight, beta_weight, query_conv, key_conv, value_conv, decay_log, decay_bias, out_gain, output_weight, hidden_gain, hidden_gate, hidden_up, hidden_down = weights
    length = x_row.shape[0]
    normed = low(rms_norm(x_row, mixer_gain))
    q_proj = low_back(matmul(normed, query_weight))
    k_proj = low_back(matmul(normed, key_weight))
    v_proj = low_back(matmul(normed, value_weight))
    z_proj = low_back(matmul(normed, gate_weight))
    a_proj = low_back(matmul(normed, decay_weight))
    b_proj = low_back(matmul(normed, beta_weight))
    seg_pad = jnp.concatenate([jnp.full((CONV - 1,), -1, jnp.int32), seg_row.astype(jnp.int32)])
    query = unit_rows(short_conv(q_proj, query_conv, seg_pad, seg_row).reshape(length, H, DK)) * DK ** (-0.5)
    keys = unit_rows(short_conv(k_proj, key_conv, seg_pad, seg_row).reshape(length, H, DK))
    values = short_conv(v_proj, value_conv, seg_pad, seg_row).reshape(length, H, DV)
    beta = jax.nn.sigmoid(b_proj)
    log_gate = -jnp.exp(decay_log) * jax.nn.softplus(a_proj + decay_bias)
    linked = (seg_pad[CONV - 2:CONV - 2 + length] == seg_row).astype(jnp.float32)
    alpha = jnp.exp(log_gate) * linked[:, None]
    core = delta_row(query, keys, values, beta, alpha)
    mixed = low((rms_norm(core, out_gain) * jax.nn.silu(z_proj.reshape(length, H, DV))).reshape(length, HV))
    attn = low_back(matmul(mixed, output_weight))
    middle = x_row + attn
    normed2 = low(rms_norm(middle, hidden_gain))
    gate_pre = low_back(matmul(normed2, hidden_gate))
    up_pre = low_back(matmul(normed2, hidden_up))
    act = low(jax.nn.silu(gate_pre) * up_pre)
    return middle + low_back(matmul(act, hidden_down))

def add_up(running, latest):
    return running + latest

def reference(tokens, segment_ids, cotangent, mixer_gain, query_weight, key_weight, value_weight, gate_weight, decay_weight, beta_weight, query_conv, key_conv, value_conv, decay_log, decay_bias, out_gain, output_weight, hidden_gain, hidden_gate, hidden_up, hidden_down):
    weights = tuple((item.astype(jnp.float32) for item in (mixer_gain, query_weight, key_weight, value_weight, gate_weight, decay_weight, beta_weight, query_conv, key_conv, value_conv, decay_log, decay_bias, out_gain, output_weight, hidden_gain, hidden_gate, hidden_up, hidden_down)))
    rows_in = tokens.astype(jnp.float32).reshape(N_SHARD, ROW, D)
    rows_cot = cotangent.astype(jnp.float32).reshape(N_SHARD, ROW, D)

    def per_row(carry, inputs):
        x_row, seg_row, cot_row = inputs

        def forward(x_value, weight_values):
            return row_forward(x_value, seg_row, weight_values)
        result, pullback = jax.vjp(forward, x_row, weights)
        grad_x, grad_weights = pullback(cot_row)
        carry = jax.tree.map(add_up, carry, grad_weights)
        return (carry, (result, grad_x))
    start_grads = jax.tree.map(jnp.zeros_like, weights)
    grads, (results, grad_rows) = lax.scan(per_row, start_grads, (rows_in, segment_ids.astype(jnp.int32), rows_cot))
    block_out = results.reshape(TOKENS, D).astype(jnp.bfloat16)
    input_grad = grad_rows.reshape(TOKENS, D)
    return (block_out, input_grad, grads[0], grads[1], grads[2], grads[3], grads[4], grads[5], grads[6], grads[7], grads[8], grads[9], grads[10], grads[11], grads[12], grads[13], grads[14], grads[15], grads[16], grads[17])
```

```python
import jax
import jax.numpy as jnp
from jax import lax
from jax.sharding import PartitionSpec as P

GROUP = 128


HIGH = lax.Precision.HIGHEST
PRECISE = lax.Precision.HIGH


def from_behind(block, axis, distance):
    devices = range(lax.axis_size(axis))
    route = [(i - distance, i) for i in devices if i - distance in devices]
    return lax.ppermute(block, axis, route)


def dot_plain(left, right):
    return jnp.dot(left, right, preferred_element_type=jnp.float32)


def dot_first(left, right):
    return lax.dot_general(
        left, right, (((0,), (0,)), ((), ())), preferred_element_type=jnp.float32
    )


def dot_second(left, right):
    return lax.dot_general(
        left, right, (((1,), (1,)), ((), ())), preferred_element_type=jnp.float32
    )


def rms_norm(values, gain):
    return values * lax.rsqrt(jnp.mean(values * values, axis=-1, keepdims=True) + 1e-06) * gain


def unit_rows(values):
    return values * lax.rsqrt(jnp.sum(values * values, axis=-1, keepdims=True) + 1e-06)


def convolve(projected, rim_rows, weights, seg_ext):
    tok_rows = projected.shape[0]
    taps = weights.shape[0]
    extended = jnp.concatenate([rim_rows, projected], axis=0)
    seg_now = seg_ext[taps - 1 :]
    summed = jnp.zeros_like(projected)
    for offset in range(taps):
        begin = taps - 1 - offset
        linked = (seg_ext[begin : begin + tok_rows] == seg_now).astype(jnp.float32)
        summed = summed + weights[offset] * extended[begin : begin + tok_rows] * linked[:, None]
    return jax.nn.silu(summed)


def dot_high(equation, left, right):
    return jnp.einsum(equation, left, right, precision=PRECISE)


@jax.custom_vjp
def unit_lower_inverse(strict_part):
    size = strict_part.shape[-1]
    order = jnp.arange(size)
    above, across = order[:, None], order[None, :]
    inverse = jnp.broadcast_to(jnp.eye(size, dtype=jnp.float32), strict_part.shape)
    width = 1
    while width < size:
        paired = (above // (2 * width) == across // (2 * width)) & (
            above // width != across // width
        )
        coupling = jnp.where(paired, strict_part, 0.0)
        if width > 1:
            coupling = dot_high("...ij,...jk->...ik", coupling, inverse)
            coupling = dot_high("...ij,...jk->...ik", inverse, coupling)
        inverse = inverse - coupling
        width *= 2
    return inverse


def inverse_keep(strict_part):
    inverse = unit_lower_inverse(strict_part)
    return inverse, inverse


def inverse_pull(inverse, grad):
    inner = dot_high("...ij,...kj->...ik", grad, inverse)
    return (-dot_high("...ji,...jk->...ik", inverse, inner),)


unit_lower_inverse.defvjp(inverse_keep, inverse_pull)


def prepare(floats, seg_ext, key_dim, block_len):
    (
        q_proj,
        k_proj,
        v_proj,
        q_rim,
        k_rim,
        v_rim,
        a_proj,
        b_proj,
        q_conv,
        k_conv,
        v_conv,
        decay_log,
        decay_bias,
    ) = floats
    tok_rows = q_proj.shape[0]
    num_heads = a_proj.shape[1]
    taps = q_conv.shape[0]
    blocks = tok_rows // block_len

    def split(array):
        shaped = array.reshape(blocks, block_len, num_heads, -1)
        return jnp.transpose(shaped, (2, 0, 1, 3))

    query = unit_rows(split(convolve(q_proj, q_rim, q_conv, seg_ext))) * key_dim ** (-0.5)
    keys = unit_rows(split(convolve(k_proj, k_rim, k_conv, seg_ext)))
    values = split(convolve(v_proj, v_rim, v_conv, seg_ext))
    val_dim = values.shape[3]
    beta = jax.nn.sigmoid(b_proj).T.reshape(num_heads, blocks, block_len)
    log_gate = (-jnp.exp(decay_log) * jax.nn.softplus(a_proj + decay_bias)).T
    log_gate = log_gate.reshape(num_heads, blocks, block_len)
    seg_now = seg_ext[taps - 1 :].reshape(blocks, block_len)
    seg_before = seg_ext[taps - 2 : taps - 2 + tok_rows : block_len]
    order = jnp.arange(block_len)
    until = (order[:, None] <= order[None, :]).astype(jnp.float32)
    cumul = jnp.einsum("hcs,st->hct", log_gate, until, precision=HIGH)
    causal = (order[:, None] >= order[None, :]) & (seg_now[:, :, None] == seg_now[:, None, :])
    strict = causal & (order[:, None] > order[None, :])
    spacing = cumul[..., :, None] - cumul[..., None, :]
    within = jnp.where(causal, jnp.exp(jnp.where(causal, spacing, 0.0)), 0.0)
    from_start = jnp.where(seg_now == seg_before[:, None], jnp.exp(cumul), 0.0)
    to_end = within[..., -1, :]
    key_dots = dot_high("hctd,hcsd->hcts", keys, keys)
    inverse = unit_lower_inverse(jnp.where(strict, beta[..., None] * within * key_dots, 0.0))
    scores = dot_high("hctd,hcsd->hcts", query, keys) * within
    sources = jnp.concatenate(
        [(beta * from_start)[..., None] * keys, beta[..., None] * values], axis=-1
    )
    solved = dot_high("hcts,hcsx->hctx", inverse, sources)
    reached = dot_high("hcts,hcsx->hctx", scores, solved)
    moved = dot_high("hctx,hctd->hcxd", solved, keys * to_end[..., None])
    eye = jnp.eye(key_dim, dtype=jnp.float32)
    step_map = from_start[..., -1][..., None, None] * eye - moved[:, :, :key_dim]
    step_base = jnp.concatenate(
        [jnp.zeros((num_heads, blocks, key_dim, key_dim), jnp.float32), moved[:, :, key_dim:]],
        axis=2,
    )
    state = jnp.concatenate(
        [
            jnp.broadcast_to(eye, (num_heads, key_dim, key_dim)),
            jnp.zeros((num_heads, val_dim, key_dim), jnp.float32),
        ],
        axis=1,
    )
    states = []
    for block in range(blocks):
        states.append(state)
        state = dot_high("hxd,hde->hxe", state, step_map[:, block]) + step_base[:, block]
    entry = jnp.stack(states, axis=1)
    reading = from_start[..., None] * query - reached[..., :key_dim]
    outputs = dot_high("hctd,hcxd->hctx", reading, entry)
    mapped = outputs[..., :key_dim].reshape(num_heads, tok_rows, key_dim)
    base = (outputs[..., key_dim:] + reached[..., key_dim:]).reshape(num_heads, tok_rows, val_dim)
    return mapped, base, state[:, :key_dim], state[:, key_dim:]


def gated_out(core, gate_proj, gain):
    num_heads, tok_rows, val_dim = core.shape
    gating = jax.nn.silu(gate_proj.reshape(tok_rows, num_heads, val_dim))
    normed = rms_norm(core, gain)
    return (jnp.transpose(normed, (1, 0, 2)) * gating).reshape(tok_rows, -1)


def swish_product(gate_pre, up_pre):
    return jax.nn.silu(gate_pre) * up_pre


def add_tail(grad_rows, incoming):
    width = incoming.shape[0]
    return jnp.concatenate([grad_rows[:-width], grad_rows[-width:] + incoming], axis=0)


def body(
    tokens,
    segment_ids,
    cotangent,
    mixer_gain,
    query_weight,
    key_weight,
    value_weight,
    gate_weight,
    decay_weight,
    beta_weight,
    query_conv,
    key_conv,
    value_conv,
    decay_log,
    decay_bias,
    out_gain,
    output_weight,
    hidden_gain,
    hidden_gate,
    hidden_up,
    hidden_down,
):
    tok_rows = tokens.shape[0]
    num_heads = decay_log.shape[0]
    key_dim = query_weight.shape[1] // num_heads
    taps = query_conv.shape[0]
    range_count = lax.axis_size("ctx")
    begin_row = lax.axis_index("ctx") * tok_rows
    seg_pad = jnp.concatenate([jnp.full((taps - 1,), -1, jnp.int32), segment_ids[0]])
    seg_ext = lax.dynamic_slice_in_dim(seg_pad, begin_row, tok_rows + taps - 1)
    low = jnp.bfloat16
    heads_wide = num_heads * key_dim
    values_wide = value_weight.shape[1]
    mixer_wide = 2 * heads_wide + 2 * values_wide
    narrow_pad = jnp.zeros((query_weight.shape[0], -2 * num_heads % 128), low)
    mixer_full = lax.all_gather(
        jnp.concatenate(
            [
                query_weight,
                key_weight,
                value_weight,
                gate_weight,
                decay_weight,
                beta_weight,
                narrow_pad,
            ],
            axis=1,
        ),
        "shard",
        axis=0,
        tiled=True,
    )
    units = hidden_gate.shape[1]
    output_full = lax.all_gather(output_weight.T, "shard", axis=0, tiled=True)
    inner_full = lax.all_gather(
        jnp.concatenate([hidden_gate, hidden_up], axis=1), "shard", axis=0, tiled=True
    )
    down_full = lax.all_gather(hidden_down.T, "shard", axis=0, tiled=True)
    part_rows = tok_rows // lax.axis_size("tp")
    part_at = lax.axis_index("tp") * part_rows

    def own_rows(array):
        return lax.dynamic_slice_in_dim(array, part_at, part_rows)

    def sum_rows(array):
        summed = lax.psum_scatter(array.astype(low), "tp", scatter_dimension=0, tiled=True)
        return summed.astype(jnp.float32)

    def all_rows(array):
        return lax.all_gather(array, "tp", axis=0, tiled=True)

    normed_low = rms_norm(tokens.astype(jnp.float32), mixer_gain).astype(low)
    x_own = own_rows(tokens).astype(jnp.float32)
    _, norm_pull = jax.vjp(rms_norm, x_own, mixer_gain)
    projected = dot_plain(normed_low, mixer_full)
    q_proj = projected[:, :heads_wide]
    k_proj = projected[:, heads_wide : 2 * heads_wide]
    v_proj = projected[:, 2 * heads_wide : 2 * heads_wide + values_wide]
    z_proj = projected[:, 2 * heads_wide + values_wide : mixer_wide]
    a_proj = projected[:, mixer_wide : mixer_wide + num_heads]
    b_proj = projected[:, mixer_wide + num_heads : mixer_wide + 2 * num_heads]
    rim = from_behind(
        projected[tok_rows - taps + 1 :, : 2 * heads_wide + values_wide], "ctx", 1
    )
    q_rim = rim[:, :heads_wide]
    k_rim = rim[:, heads_wide : 2 * heads_wide]
    v_rim = rim[:, 2 * heads_wide :]

    def local_mixer(floats):
        return prepare(floats, seg_ext, key_dim, GROUP)

    (mapped_query, base_query, state_map, state_base), prep_pull = jax.vjp(
        local_mixer,
        (
            q_proj,
            k_proj,
            v_proj,
            q_rim,
            k_rim,
            v_rim,
            a_proj,
            b_proj,
            query_conv,
            key_conv,
            value_conv,
            decay_log,
            decay_bias,
        ),
    )
    state_in = jnp.zeros_like(state_base)
    for _ in range(range_count - 1):
        ends = dot_high("hvd,hde->hve", state_in, state_map) + state_base
        state_in = from_behind(ends, "ctx", 1)
    core = base_query + dot_high("hrd,hvd->hrv", mapped_query, state_in)
    mixed, post_pull = jax.vjp(gated_out, core, z_proj, out_gain)
    mixed_low = mixed.astype(low)
    middle = x_own + sum_rows(dot_second(mixed_low, output_full))
    normed2, norm2_pull = jax.vjp(rms_norm, middle, hidden_gain)
    normed2_low = all_rows(normed2.astype(low))
    inner = dot_plain(normed2_low, inner_full)
    act, act_pull = jax.vjp(swish_product, inner[:, :units], inner[:, units:])
    act_low = act.astype(low)
    grad_act = dot_plain(cotangent, down_full)
    grad_gate, grad_up = act_pull(grad_act)
    inner_low = jnp.concatenate([grad_gate.astype(low), grad_up.astype(low)], axis=1)
    grad_normed2 = sum_rows(dot_second(inner_low, inner_full))
    ffn = sum_rows(dot_second(act_low, down_full))
    block_out = all_rows((middle + ffn).astype(low))
    grad_down = dot_first(cotangent, act_low)
    grad_inner = dot_first(normed2_low, inner_low)
    grad_mid_norm, grad_hidden_gain = norm2_pull(grad_normed2)
    grad_middle = own_rows(cotangent).astype(jnp.float32) + grad_mid_norm
    attn_low = all_rows(grad_middle.astype(low))
    grad_output = dot_first(attn_low, mixed_low)
    grad_mixed = dot_plain(attn_low, output_full)
    grad_core, grad_z, grad_out_gain = post_pull(grad_mixed)
    direct = dot_high("hrv,hrd->hvd", grad_core, mapped_query)
    grad_end = jnp.zeros_like(direct)
    for _ in range(range_count - 1):
        totals = dot_high("hve,hde->hvd", grad_end, state_map) + direct
        grad_end = from_behind(totals.astype(low), "ctx", -1).astype(totals.dtype)
    grad_mapped = dot_high("hrv,hvd->hrd", grad_core, state_in)
    grad_map = dot_high("hvd,hve->hde", state_in, grad_end)
    (float_grads,) = prep_pull((grad_mapped, grad_core, grad_map, grad_end))
    (
        grad_q,
        grad_k,
        grad_v,
        grad_q_rim,
        grad_k_rim,
        grad_v_rim,
        grad_a,
        grad_b,
        grad_q_conv,
        grad_k_conv,
        grad_v_conv,
        grad_decay_log,
        grad_decay_bias,
    ) = float_grads
    back_rim = from_behind(
        jnp.concatenate([grad_q_rim, grad_k_rim, grad_v_rim], axis=1), "ctx", -1
    )
    conv_grad = add_tail(jnp.concatenate([grad_q, grad_k, grad_v], axis=1), back_rim)
    mixer_low = jnp.concatenate(
        [
            conv_grad.astype(low),
            grad_z.astype(low),
            grad_a.astype(low),
            grad_b.astype(low),
            jnp.zeros((tok_rows, narrow_pad.shape[1]), low),
        ],
        axis=1,
    )
    grad_normed = sum_rows(dot_second(mixer_low, mixer_full))
    grad_mixer = dot_first(normed_low, mixer_low)
    grad_x_norm, grad_mixer_gain = norm_pull(grad_normed)
    input_grad = all_rows((grad_middle + grad_x_norm).astype(low)).astype(jnp.float32)

    def sum_weight(array):
        part = lax.psum_scatter(array.astype(low), "shard", scatter_dimension=0, tiled=True)
        return lax.psum(part, "ctx").astype(jnp.float32)

    sum_inner = sum_weight(jnp.concatenate([grad_inner, grad_down, grad_output], axis=1))
    sum_mixer = sum_weight(grad_mixer)
    sum_mixer_gain, sum_hidden_gain, sum_out_gain = lax.psum(
        (grad_mixer_gain, grad_hidden_gain, grad_out_gain), ("shard", "ctx", "tp")
    )
    sum_q_conv, sum_k_conv, sum_v_conv, sum_decay_log, sum_decay_bias = lax.psum(
        (grad_q_conv, grad_k_conv, grad_v_conv, grad_decay_log, grad_decay_bias),
        ("shard", "ctx"),
    )
    return (
        block_out,
        input_grad,
        sum_mixer_gain,
        sum_mixer[:, :heads_wide],
        sum_mixer[:, heads_wide : 2 * heads_wide],
        sum_mixer[:, 2 * heads_wide : 2 * heads_wide + values_wide],
        sum_mixer[:, 2 * heads_wide + values_wide : mixer_wide],
        sum_mixer[:, mixer_wide : mixer_wide + num_heads],
        sum_mixer[:, mixer_wide + num_heads : mixer_wide + 2 * num_heads],
        sum_q_conv,
        sum_k_conv,
        sum_v_conv,
        sum_decay_log,
        sum_decay_bias,
        sum_out_gain,
        sum_inner[:, 3 * units :].T,
        sum_hidden_gain,
        sum_inner[:, :units],
        sum_inner[:, units : 2 * units],
        sum_inner[:, 2 * units : 3 * units].T,
    )


def solution(mesh):
    in_specs = (
        P(("shard", "ctx"), None),
        P("shard", None),
        P(("shard", "ctx"), None),
        P(),
        P("shard", "tp"),
        P("shard", "tp"),
        P("shard", "tp"),
        P("shard", "tp"),
        P("shard", "tp"),
        P("shard", "tp"),
        P(None, "tp"),
        P(None, "tp"),
        P(None, "tp"),
        P("tp"),
        P("tp"),
        P(),
        P("tp", "shard"),
        P(),
        P("shard", "tp"),
        P("shard", "tp"),
        P("tp", "shard"),
    )
    out_specs = (
        P(("shard", "ctx"), None),
        P(("shard", "ctx"), None),
        P(),
        P("shard", "tp"),
        P("shard", "tp"),
        P("shard", "tp"),
        P("shard", "tp"),
        P("shard", "tp"),
        P("shard", "tp"),
        P(None, "tp"),
        P(None, "tp"),
        P(None, "tp"),
        P("tp"),
        P("tp"),
        P(),
        P("tp", "shard"),
        P(),
        P("shard", "tp"),
        P("shard", "tp"),
        P("tp", "shard"),
    )
    return jax.shard_map(body, mesh=mesh, in_specs=in_specs, out_specs=out_specs, check_vma=False)
```

```python
import jax
import jax.numpy as jnp
from jax import lax
from jax.sharding import PartitionSpec as P

GROUP = 128


HIGH = lax.Precision.HIGHEST
PRECISE = lax.Precision.HIGH


def from_behind(block, axis, distance):
    devices = range(lax.axis_size(axis))
    route = [(i - distance, i) for i in devices if i - distance in devices]
    return lax.ppermute(block, axis, route)


def dot_plain(left, right):
    return jnp.dot(left, right, preferred_element_type=jnp.float32)


def dot_first(left, right):
    return lax.dot_general(
        left, right, (((0,), (0,)), ((), ())), preferred_element_type=jnp.float32
    )


def dot_second(left, right):
    return lax.dot_general(
        left, right, (((1,), (1,)), ((), ())), preferred_element_type=jnp.float32
    )


def rms_norm(values, gain):
    return values * lax.rsqrt(jnp.mean(values * values, axis=-1, keepdims=True) + 1e-06) * gain


def unit_rows(values):
    return values * lax.rsqrt(jnp.sum(values * values, axis=-1, keepdims=True) + 1e-06)


def convolve(projected, rim_rows, weights, seg_ext):
    tok_rows = projected.shape[0]
    taps = weights.shape[0]
    extended = jnp.concatenate([rim_rows, projected], axis=0)
    seg_now = seg_ext[taps - 1 :]
    summed = jnp.zeros_like(projected)
    for offset in range(taps):
        begin = taps - 1 - offset
        linked = (seg_ext[begin : begin + tok_rows] == seg_now).astype(jnp.float32)
        summed = summed + weights[offset] * extended[begin : begin + tok_rows] * linked[:, None]
    return jax.nn.silu(summed)


def dot_high(equation, left, right):
    return jnp.einsum(equation, left, right, precision=PRECISE)


@jax.custom_vjp
def unit_lower_inverse(strict_part):
    size = strict_part.shape[-1]
    order = jnp.arange(size)
    above, across = order[:, None], order[None, :]
    inverse = jnp.broadcast_to(jnp.eye(size, dtype=jnp.float32), strict_part.shape)
    width = 1
    while width < size:
        paired = (above // (2 * width) == across // (2 * width)) & (
            above // width != across // width
        )
        coupling = jnp.where(paired, strict_part, 0.0)
        if width > 1:
            coupling = dot_high("...ij,...jk->...ik", coupling, inverse)
            coupling = dot_high("...ij,...jk->...ik", inverse, coupling)
        inverse = inverse - coupling
        width *= 2
    return inverse


def inverse_keep(strict_part):
    inverse = unit_lower_inverse(strict_part)
    return inverse, inverse


def inverse_pull(inverse, grad):
    inner = dot_high("...ij,...kj->...ik", grad, inverse)
    return (-dot_high("...ji,...jk->...ik", inverse, inner),)


unit_lower_inverse.defvjp(inverse_keep, inverse_pull)


def prepare(floats, seg_ext, key_dim, block_len):
    (
        q_proj,
        k_proj,
        v_proj,
        q_rim,
        k_rim,
        v_rim,
        a_proj,
        b_proj,
        q_conv,
        k_conv,
        v_conv,
        decay_log,
        decay_bias,
    ) = floats
    tok_rows = q_proj.shape[0]
    num_heads = a_proj.shape[1]
    taps = q_conv.shape[0]
    blocks = tok_rows // block_len

    def split(array):
        shaped = array.reshape(blocks, block_len, num_heads, -1)
        return jnp.transpose(shaped, (2, 0, 1, 3))

    query = unit_rows(split(convolve(q_proj, q_rim, q_conv, seg_ext))) * key_dim ** (-0.5)
    keys = unit_rows(split(convolve(k_proj, k_rim, k_conv, seg_ext)))
    values = split(convolve(v_proj, v_rim, v_conv, seg_ext))
    val_dim = values.shape[3]
    beta = jax.nn.sigmoid(b_proj).T.reshape(num_heads, blocks, block_len)
    log_gate = (-jnp.exp(decay_log) * jax.nn.softplus(a_proj + decay_bias)).T
    log_gate = log_gate.reshape(num_heads, blocks, block_len)
    seg_now = seg_ext[taps - 1 :].reshape(blocks, block_len)
    seg_before = seg_ext[taps - 2 : taps - 2 + tok_rows : block_len]
    order = jnp.arange(block_len)
    until = (order[:, None] <= order[None, :]).astype(jnp.float32)
    cumul = jnp.einsum("hcs,st->hct", log_gate, until, precision=HIGH)
    causal = (order[:, None] >= order[None, :]) & (seg_now[:, :, None] == seg_now[:, None, :])
    strict = causal & (order[:, None] > order[None, :])
    spacing = cumul[..., :, None] - cumul[..., None, :]
    within = jnp.where(causal, jnp.exp(jnp.where(causal, spacing, 0.0)), 0.0)
    from_start = jnp.where(seg_now == seg_before[:, None], jnp.exp(cumul), 0.0)
    to_end = within[..., -1, :]
    key_dots = dot_high("hctd,hcsd->hcts", keys, keys)
    inverse = unit_lower_inverse(jnp.where(strict, beta[..., None] * within * key_dots, 0.0))
    scores = dot_high("hctd,hcsd->hcts", query, keys) * within
    sources = jnp.concatenate(
        [(beta * from_start)[..., None] * keys, beta[..., None] * values], axis=-1
    )
    solved = dot_high("hcts,hcsx->hctx", inverse, sources)
    reached = dot_high("hcts,hcsx->hctx", scores, solved)
    moved = dot_high("hctx,hctd->hcxd", solved, keys * to_end[..., None])
    eye = jnp.eye(key_dim, dtype=jnp.float32)
    step_map = from_start[..., -1][..., None, None] * eye - moved[:, :, :key_dim]
    step_base = jnp.concatenate(
        [jnp.zeros((num_heads, blocks, key_dim, key_dim), jnp.float32), moved[:, :, key_dim:]],
        axis=2,
    )
    state = jnp.concatenate(
        [
            jnp.broadcast_to(eye, (num_heads, key_dim, key_dim)),
            jnp.zeros((num_heads, val_dim, key_dim), jnp.float32),
        ],
        axis=1,
    )
    states = []
    for block in range(blocks):
        states.append(state)
        state = dot_high("hxd,hde->hxe", state, step_map[:, block]) + step_base[:, block]
    entry = jnp.stack(states, axis=1)
    reading = from_start[..., None] * query - reached[..., :key_dim]
    outputs = dot_high("hctd,hcxd->hctx", reading, entry)
    mapped = outputs[..., :key_dim].reshape(num_heads, tok_rows, key_dim)
    base = (outputs[..., key_dim:] + reached[..., key_dim:]).reshape(num_heads, tok_rows, val_dim)
    return mapped, base, state[:, :key_dim], state[:, key_dim:]


def gated_out(core, gate_proj, gain):
    num_heads, tok_rows, val_dim = core.shape
    gating = jax.nn.silu(gate_proj.reshape(tok_rows, num_heads, val_dim))
    normed = rms_norm(core, gain)
    return (jnp.transpose(normed, (1, 0, 2)) * gating).reshape(tok_rows, -1)


def swish_product(gate_pre, up_pre):
    return jax.nn.silu(gate_pre) * up_pre


def add_tail(grad_rows, incoming):
    width = incoming.shape[0]
    return jnp.concatenate([grad_rows[:-width], grad_rows[-width:] + incoming], axis=0)


def body(
    tokens,
    segment_ids,
    cotangent,
    mixer_gain,
    query_weight,
    key_weight,
    value_weight,
    gate_weight,
    decay_weight,
    beta_weight,
    query_conv,
    key_conv,
    value_conv,
    decay_log,
    decay_bias,
    out_gain,
    output_weight,
    hidden_gain,
    hidden_gate,
    hidden_up,
    hidden_down,
):
    tok_rows = tokens.shape[0]
    num_heads = decay_log.shape[0]
    key_dim = query_weight.shape[1] // num_heads
    taps = query_conv.shape[0]
    range_count = lax.axis_size("ctx")
    begin_row = lax.axis_index("ctx") * tok_rows
    seg_pad = jnp.concatenate([jnp.full((taps - 1,), -1, jnp.int32), segment_ids[0]])
    seg_ext = lax.dynamic_slice_in_dim(seg_pad, begin_row, tok_rows + taps - 1)
    low = jnp.bfloat16
    heads_wide = num_heads * key_dim
    values_wide = value_weight.shape[1]
    mixer_wide = 2 * heads_wide + 2 * values_wide
    narrow_pad = jnp.zeros((query_weight.shape[0], -(mixer_wide + 2 * num_heads) % 256), low)
    paired = range_count == 2
    partner = [(0, 1), (1, 0)]
    core = lax.axis_index("ctx")

    def swap(array):
        return lax.ppermute(array, "ctx", partner)

    def joined(own_half, other_half):
        ahead = jnp.where(core == 0, own_half, other_half)
        behind = jnp.where(core == 0, other_half, own_half)
        return jnp.concatenate([ahead, behind], axis=1)

    def half_of(array, index):
        half = array.shape[1] // 2
        return lax.dynamic_slice_in_dim(array, index * half, half, axis=1)

    def gather_weight(array):
        if not paired:
            return lax.all_gather(array, "shard", axis=0, tiled=True)
        own_half = lax.all_gather(half_of(array, core), "shard", axis=0, tiled=True)
        return joined(own_half, swap(own_half))

    def sum_weight(array):
        array = array.astype(low)
        if not paired:
            part = lax.psum_scatter(array, "shard", scatter_dimension=0, tiled=True)
            return lax.psum(part, "ctx").astype(jnp.float32)
        incoming = swap(half_of(array, 1 - core))
        own_half = half_of(array, core).astype(jnp.float32) + incoming.astype(jnp.float32)
        part = lax.psum_scatter(own_half.astype(low), "shard", scatter_dimension=0, tiled=True)
        return joined(part, swap(part)).astype(jnp.float32)

    mixer_full = gather_weight(
        jnp.concatenate(
            [
                query_weight,
                key_weight,
                value_weight,
                gate_weight,
                decay_weight,
                beta_weight,
                narrow_pad,
            ],
            axis=1,
        )
    )
    units = hidden_gate.shape[1]
    later_wide = 3 * units + values_wide
    later_pad = jnp.zeros((query_weight.shape[0], -later_wide % 256), low)
    later_full = gather_weight(
        jnp.concatenate(
            [hidden_gate, hidden_up, hidden_down.T, output_weight.T, later_pad], axis=1
        )
    )
    part_rows = tok_rows // lax.axis_size("tp")
    part_at = lax.axis_index("tp") * part_rows

    def own_rows(array):
        return lax.dynamic_slice_in_dim(array, part_at, part_rows)

    def sum_rows(array):
        summed = lax.psum_scatter(array.astype(low), "tp", scatter_dimension=0, tiled=True)
        return summed.astype(jnp.float32)

    def all_rows(array):
        return lax.all_gather(array, "tp", axis=0, tiled=True)

    normed_low = rms_norm(tokens.astype(jnp.float32), mixer_gain).astype(low)
    x_own = own_rows(tokens).astype(jnp.float32)
    _, norm_pull = jax.vjp(rms_norm, x_own, mixer_gain)
    projected = dot_plain(normed_low, mixer_full)
    q_proj = projected[:, :heads_wide]
    k_proj = projected[:, heads_wide : 2 * heads_wide]
    v_proj = projected[:, 2 * heads_wide : 2 * heads_wide + values_wide]
    z_proj = projected[:, 2 * heads_wide + values_wide : mixer_wide]
    a_proj = projected[:, mixer_wide : mixer_wide + num_heads]
    b_proj = projected[:, mixer_wide + num_heads : mixer_wide + 2 * num_heads]
    rim = from_behind(
        projected[tok_rows - taps + 1 :, : 2 * heads_wide + values_wide], "ctx", 1
    )
    q_rim = rim[:, :heads_wide]
    k_rim = rim[:, heads_wide : 2 * heads_wide]
    v_rim = rim[:, 2 * heads_wide :]

    def local_mixer(floats):
        return prepare(floats, seg_ext, key_dim, GROUP)

    (mapped_query, base_query, state_map, state_base), prep_pull = jax.vjp(
        local_mixer,
        (
            q_proj,
            k_proj,
            v_proj,
            q_rim,
            k_rim,
            v_rim,
            a_proj,
            b_proj,
            query_conv,
            key_conv,
            value_conv,
            decay_log,
            decay_bias,
        ),
    )
    state_in = jnp.zeros_like(state_base)
    for _ in range(range_count - 1):
        ends = dot_high("hvd,hde->hve", state_in, state_map) + state_base
        state_in = from_behind(ends, "ctx", 1)
    heads_out = base_query + dot_high("hrd,hvd->hrv", mapped_query, state_in)
    mixed, post_pull = jax.vjp(gated_out, heads_out, z_proj, out_gain)
    mixed_low, later_full = lax.optimization_barrier((mixed.astype(low), later_full))
    inner_full = later_full[:, : 2 * units]
    down_full = later_full[:, 2 * units : 3 * units]
    output_full = later_full[:, 3 * units : later_wide]
    middle = x_own + sum_rows(dot_second(mixed_low, output_full))
    normed2, norm2_pull = jax.vjp(rms_norm, middle, hidden_gain)
    normed2_low = all_rows(normed2.astype(low))
    inner = dot_plain(normed2_low, inner_full)
    act, act_pull = jax.vjp(swish_product, inner[:, :units], inner[:, units:])
    act_low = act.astype(low)
    grad_act = dot_plain(cotangent, down_full)
    grad_gate, grad_up = act_pull(grad_act)
    inner_low = jnp.concatenate([grad_gate.astype(low), grad_up.astype(low)], axis=1)
    grad_normed2 = sum_rows(dot_second(inner_low, inner_full))
    grad_mid_norm, grad_hidden_gain = norm2_pull(grad_normed2)
    grad_middle = own_rows(cotangent).astype(jnp.float32) + grad_mid_norm
    attn_low = all_rows(grad_middle.astype(low))
    act_late, attn_low = lax.optimization_barrier((act_low, attn_low))
    ffn = sum_rows(dot_second(act_late, down_full))
    block_out = all_rows((middle + ffn).astype(low))
    grad_down = dot_first(cotangent, act_low)
    grad_inner = dot_first(normed2_low, inner_low)
    grad_output = dot_first(attn_low, mixed_low)
    later_zeros = jnp.zeros((tokens.shape[1], later_pad.shape[1]), jnp.float32)
    sum_later = sum_weight(
        jnp.concatenate([grad_inner, grad_down, grad_output, later_zeros], axis=1)
    )
    grad_mixed = dot_plain(attn_low, output_full)
    grad_core, grad_z, grad_out_gain = post_pull(grad_mixed)
    direct = dot_high("hrv,hrd->hvd", grad_core, mapped_query)
    grad_end = jnp.zeros_like(direct)
    for _ in range(range_count - 1):
        totals = dot_high("hve,hde->hvd", grad_end, state_map) + direct
        grad_end = from_behind(totals.astype(low), "ctx", -1).astype(totals.dtype)
    grad_mapped = dot_high("hrv,hvd->hrd", grad_core, state_in)
    grad_map = dot_high("hvd,hve->hde", state_in, grad_end)
    (float_grads,) = prep_pull((grad_mapped, grad_core, grad_map, grad_end))
    (
        grad_q,
        grad_k,
        grad_v,
        grad_q_rim,
        grad_k_rim,
        grad_v_rim,
        grad_a,
        grad_b,
        grad_q_conv,
        grad_k_conv,
        grad_v_conv,
        grad_decay_log,
        grad_decay_bias,
    ) = float_grads
    back_rim = from_behind(
        jnp.concatenate([grad_q_rim, grad_k_rim, grad_v_rim], axis=1), "ctx", -1
    )
    conv_grad = add_tail(jnp.concatenate([grad_q, grad_k, grad_v], axis=1), back_rim)
    mixer_low = jnp.concatenate(
        [
            conv_grad.astype(low),
            grad_z.astype(low),
            grad_a.astype(low),
            grad_b.astype(low),
            jnp.zeros((tok_rows, narrow_pad.shape[1]), low),
        ],
        axis=1,
    )
    mixer_low, block_out, sum_later = lax.optimization_barrier((mixer_low, block_out, sum_later))
    grad_normed = sum_rows(dot_second(mixer_low, mixer_full))
    grad_mixer = dot_first(normed_low, mixer_low)
    grad_x_norm, grad_mixer_gain = norm_pull(grad_normed)
    input_grad = all_rows((grad_middle + grad_x_norm).astype(low)).astype(jnp.float32)

    sum_mixer = sum_weight(grad_mixer)
    sum_mixer_gain, sum_hidden_gain, sum_out_gain = lax.psum(
        (grad_mixer_gain, grad_hidden_gain, grad_out_gain), ("shard", "ctx", "tp")
    )
    sum_q_conv, sum_k_conv, sum_v_conv, sum_decay_log, sum_decay_bias = lax.psum(
        (grad_q_conv, grad_k_conv, grad_v_conv, grad_decay_log, grad_decay_bias),
        ("shard", "ctx"),
    )
    return (
        block_out,
        input_grad,
        sum_mixer_gain,
        sum_mixer[:, :heads_wide],
        sum_mixer[:, heads_wide : 2 * heads_wide],
        sum_mixer[:, 2 * heads_wide : 2 * heads_wide + values_wide],
        sum_mixer[:, 2 * heads_wide + values_wide : mixer_wide],
        sum_mixer[:, mixer_wide : mixer_wide + num_heads],
        sum_mixer[:, mixer_wide + num_heads : mixer_wide + 2 * num_heads],
        sum_q_conv,
        sum_k_conv,
        sum_v_conv,
        sum_decay_log,
        sum_decay_bias,
        sum_out_gain,
        sum_later[:, 3 * units : later_wide].T,
        sum_hidden_gain,
        sum_later[:, :units],
        sum_later[:, units : 2 * units],
        sum_later[:, 2 * units : 3 * units].T,
    )


def solution(mesh):
    in_specs = (
        P(("shard", "ctx"), None),
        P("shard", None),
        P(("shard", "ctx"), None),
        P(),
        P("shard", "tp"),
        P("shard", "tp"),
        P("shard", "tp"),
        P("shard", "tp"),
        P("shard", "tp"),
        P("shard", "tp"),
        P(None, "tp"),
        P(None, "tp"),
        P(None, "tp"),
        P("tp"),
        P("tp"),
        P(),
        P("tp", "shard"),
        P(),
        P("shard", "tp"),
        P("shard", "tp"),
        P("tp", "shard"),
    )
    out_specs = (
        P(("shard", "ctx"), None),
        P(("shard", "ctx"), None),
        P(),
        P("shard", "tp"),
        P("shard", "tp"),
        P("shard", "tp"),
        P("shard", "tp"),
        P("shard", "tp"),
        P("shard", "tp"),
        P(None, "tp"),
        P(None, "tp"),
        P(None, "tp"),
        P("tp"),
        P("tp"),
        P(),
        P("tp", "shard"),
        P(),
        P("shard", "tp"),
        P("shard", "tp"),
        P("tp", "shard"),
    )
    return jax.shard_map(body, mesh=mesh, in_specs=in_specs, out_specs=out_specs, check_vma=False)
```
